32 devices in a mesh: grp: 4 (over z), ori: 8 (over y, x, core).
Axes of the slice: x: 2, y: 2, z: 4, core: 2. Of those that a mesh axis runs over, the one named last changes fastest.
Arguments:
- particles: bfloat16 [1024, 16640], P(('grp', 'ori')), may hold values from -8 to 8
- priors: int32 [1024, 2], P(('grp', 'ori')), may hold values from 0 to 7, all different within a row; in each aligned block of 32 rows (0 to 31, 32 to 63, ...) at most 16 rows name the same one
- offsets: int32 [2, 1024], P(None, ('grp', 'ori')), may hold values from -2 to 2
- classes: int32 [1024], P(('grp', 'ori')), may hold values from 0 to 15
- ctf_table: float32 [16, 8320], replicated, may hold values from 0.2 to 1
- references: bfloat16 [128, 16640], P('ori'), may hold values from -5 to 5
Outputs:
- back_sum: float32 [128, 16640], P('ori', 'grp')
- ctf_weight: float32 [128, 8320], P('ori', 'grp')
- log_evidence: float32 [1024], P(('grp', 'ori'))
The draws below stay inside these ranges and needn't reach their ends.
Inputs may be any that keep to these rules, and one draw needn't show every extreme that they name: `priors`: each particle names 2 different orientation blocks. The 32 rows of one device name any one block at most 16 times, and some block is named exactly 16 times by the rows of some devices.
All inputs are finite; a program needn't handle non-finite values.
Results may differ from the reference program's by a relative error of at most 0.0052.
Values may be sent and summed in bfloat16 or wider, within the bound.
A program may use at most 64 MiB of HBM per device.

```python
import math
import jax
import jax.numpy as jnp
import numpy as np
from jax import lax

PX = 128
PY = 65
BOX = 320
PIX = 8320
KD = 16640
SIDE = 8
NSHIFT = 64
K_PRI = 2
NCLASS = 16
R_DEV = 16
P_DEV = 32
CAP = 16
R_ALL = 128
PARTICLES = 1024
N_GRP = 4
N_ORI = 8


def draw_references(key, part):
    noise_part = jnp.clip(jax.random.normal(jax.random.fold_in(key, 202), (R_ALL, KD), jnp.float32), -5.0, 5.0)
    values = noise_part
    return values.astype(jnp.bfloat16)


def draw_particles(key, part):
    noise_part = jnp.clip(jax.random.normal(jax.random.fold_in(key, 303), (PARTICLES, KD), jnp.float32), -4.0, 4.0)
    values = noise_part
    return values.astype(jnp.bfloat16)


def touch_ends(array, stream_key, low, top_value):
    extent = array.shape
    index_at = [jax.random.randint(jax.random.fold_in(stream_key, axis), (), 0, extent[axis]) for axis in range(len(extent))]
    array = array.at[tuple(index_at)].set(low)
    longest = extent.index(max(extent))
    index_at[longest] = (index_at[longest] + 1) % extent[longest]
    return array.at[tuple(index_at)].set(top_value)


def assign_block(own_key, own, number, rows, amount, top, most, lean):
    order = jax.random.permutation(own_key, amount)
    packed, usual = load_shares(amount, rows * top, most, lean, True), load_shares(amount, rows * top, most, lean, False)
    places = jnp.arange(amount)

    def named(lengths, offset_by):
        used = int((lengths > 0).sum())
        fixed = max(1, used // 4)
        passed = fixed + (places - fixed + offset_by * (used - fixed)) % max(1, amount - fixed)
        return jnp.zeros((amount,), jnp.int32).at[order[jnp.where(places < fixed, places, passed)]].set(jnp.asarray(lengths, jnp.int32))

    lengths = jnp.where(number % 4 == 0, named(packed, number // 4), named(usual, number - number // 4 - 1))
    mixed = jax.random.permutation(jax.random.fold_in(own, 3), amount)
    giver, receiver = mixed[0:amount // 2 * 2:2], mixed[1:amount // 2 * 2:2]
    slack = jnp.minimum(lengths[giver] - 1, most - lengths[receiver]) // 2
    slack = jnp.where((giver == order[0]) | (receiver == order[0]) | (lengths[receiver] == 0), 0, jnp.maximum(slack, 0))
    passed = jax.random.randint(jax.random.fold_in(own, 4), (amount // 2,), 0, 1 << 20) % (slack + 1)
    lengths = lengths.at[giver].add(-passed).at[receiver].add(passed)
    items = jnp.searchsorted(jnp.cumsum(lengths), jnp.arange(rows * top), side="right").astype(jnp.int32)
    listing = items.reshape(top, rows).T
    listing = listing[jax.random.permutation(jax.random.fold_in(own, 1), rows)]
    offset_by = jax.random.randint(jax.random.fold_in(own, 2), (rows, 1), 0, top)
    return jnp.take_along_axis(listing, (jnp.arange(top)[None, :] + offset_by) % top, axis=1)


def load_shares(number_of, total, reach, slope, full):
    weights = [(1 << 20) // math.isqrt(grade ** slope) + 1 for grade in range(1, number_of + 1)]
    largest = reach if full else min(reach, max(-(-total // number_of), total * weights[0] // sum(weights)))
    least = 1 if total - largest >= number_of - 1 else 0
    holding, rest = [largest] + [least] * (number_of - 1), total - largest - least * (number_of - 1)
    while rest > 0:
        candidates = [i for i in range(1, number_of) if holding[i] < largest] or [i for i in range(1, number_of) if holding[i] < reach]
        mass, remaining = sum([weights[i] for i in candidates]), rest
        for i in candidates:
            extra = min(reach - holding[i], max(1, remaining * weights[i] // mass), rest)
            holding[i] = holding[i] + extra
            rest = rest - extra
    return np.array(holding)


def setup_inputs(seed: int = 0) -> dict:
    keys = jax.random.split(jax.random.key(seed), 7)
    particles = draw_particles(jax.random.fold_in(keys[6], 71), 0)
    priors_keys = jax.random.split(jax.random.fold_in(keys[1], 1), PARTICLES // P_DEV)
    priors_turns = jax.random.permutation(jax.random.fold_in(keys[1], 3), PARTICLES // P_DEV)
    priors = jax.vmap(lambda own, number: assign_block(jax.random.fold_in(keys[1], 2), own, number, P_DEV, N_ORI, K_PRI, CAP, 2))(priors_keys, priors_turns).reshape((PARTICLES, K_PRI))
    offsets = touch_ends(jax.random.randint(keys[2], (2, PARTICLES), -2, 3), jax.random.fold_in(keys[2], 1), -2, 2).astype(jnp.int32)
    classes = touch_ends(jax.random.randint(keys[3], (PARTICLES,), 0, NCLASS), jax.random.fold_in(keys[3], 1), 0, NCLASS - 1).astype(jnp.int32)
    ctf_table = jnp.clip(jnp.exp(jax.random.uniform(keys[4], (NCLASS, PIX), jnp.float32, math.log(0.2), math.log(1.0))), 0.2, 1.0)
    references = draw_references(jax.random.fold_in(keys[6], 71), 0)
    return dict(particles=particles, priors=priors, offsets=offsets, classes=classes, ctf_table=ctf_table, references=references)


two_pi = 2.0 * math.pi

def frequencies():
    row_ids = jnp.arange(PX)
    freq_x = jnp.where(row_ids < PX // 2, row_ids, row_ids - PX).astype(jnp.float32)
    freq_y = jnp.arange(PY).astype(jnp.float32)
    return (jnp.repeat(freq_x, PY), jnp.tile(freq_y, PX))

def phases(shift_x, shift_y):
    freq_x, freq_y = frequencies()
    angle_grid = two_pi * (shift_x[:, None] * freq_x[None, :] + shift_y[:, None] * freq_y[None, :]) / BOX
    return (jnp.cos(angle_grid), jnp.sin(angle_grid))

def grid_shifts(first_shift, shift_count):
    shift_ids = first_shift + jnp.arange(shift_count)
    return ((shift_ids // SIDE - SIDE // 2).astype(jnp.float32), (shift_ids % SIDE - SIDE // 2).astype(jnp.float32))

def kernel_of(block_refs, cosine, sine_table):
    pixel_count = PX * PY
    real_part = block_refs[:, :pixel_count].astype(jnp.float32)
    imag_part = block_refs[:, pixel_count:].astype(jnp.float32)
    left_half = cosine[:, None, :] * real_part[None] - sine_table[:, None, :] * imag_part[None]
    right_half = sine_table[:, None, :] * real_part[None] + cosine[:, None, :] * imag_part[None]
    joined = jnp.concatenate([left_half, right_half], axis=-1)
    return joined.reshape(cosine.shape[0] * block_refs.shape[0], 2 * pixel_count).astype(jnp.bfloat16)

def reference(particles, priors, offsets, classes, ctf_table, references):
    pixel_count = PX * PY
    score_scale = 2.0 / math.sqrt(pixel_count)
    ctf_rows_all = ctf_table[classes]
    cosine, sine_table = phases(offsets[0].astype(jnp.float32), offsets[1].astype(jnp.float32))
    real_part = particles[:, :pixel_count].astype(jnp.float32)
    imag_part = particles[:, pixel_count:].astype(jnp.float32)
    shifted = jnp.concatenate([ctf_rows_all * (real_part * cosine + imag_part * sine_table), ctf_rows_all * (imag_part * cosine - real_part * sine_table)], axis=-1).astype(jnp.bfloat16)
    grid_x, grid_y = grid_shifts(0, NSHIFT)
    grid_cos, grid_sin = phases(grid_x, grid_y)
    flat_priors = priors.reshape(-1)
    block_room = N_GRP * N_ORI * CAP
    ref_blocks = references.reshape(N_ORI, R_DEV, 2 * pixel_count)
    owners = jnp.arange(N_ORI, dtype=jnp.int32)

    def select_copies(owner_id):
        named_mask = flat_priors == owner_id
        copy_ids = jnp.nonzero(named_mask, size=block_room, fill_value=0)[0].astype(jnp.int32)
        valid_rows = jnp.arange(block_room) < jnp.sum(named_mask.astype(jnp.int32))
        return (copy_ids, valid_rows, copy_ids // K_PRI)

    def scores_of(owner_id, block_refs):
        copy_ids, valid_rows, row_ids = select_copies(owner_id)
        kernel_rows = kernel_of(block_refs, grid_cos, grid_sin)
        rows_data = shifted[row_ids]
        scores = jnp.dot(rows_data, kernel_rows.T, preferred_element_type=jnp.float32) * score_scale
        return (copy_ids, valid_rows, row_ids, rows_data, scores)

    def first_pass(inputs):
        owner_id, block_refs = inputs
        copy_ids, valid_rows, row_ids, rows_data, scores = scores_of(owner_id, block_refs)
        top_score = lax.optimization_barrier(jnp.max(scores, axis=1))
        copy_lse = top_score + jnp.log(lax.optimization_barrier(jnp.sum(jnp.exp(scores - top_score[:, None]), axis=1)))
        return (copy_ids, jnp.where(valid_rows, copy_lse, 0.0))
    ids_all, lse_all = lax.map(first_pass, (owners, ref_blocks))
    copy_lse = jnp.zeros((flat_priors.shape[0],), jnp.float32).at[ids_all.reshape(-1)].add(lse_all.reshape(-1))
    copy_lse = copy_lse.reshape(-1, K_PRI)
    top_copy = lax.optimization_barrier(jnp.max(copy_lse, axis=1))
    evidence = top_copy + jnp.log(lax.optimization_barrier(jnp.sum(jnp.exp(copy_lse - top_copy[:, None]), axis=1)))

    def second_pass(inputs):
        owner_id, block_refs = inputs
        copy_ids, valid_rows, row_ids, rows_data, scores = scores_of(owner_id, block_refs)
        weights = jnp.exp(scores - evidence[row_ids][:, None]) * valid_rows.astype(jnp.float32)[:, None]
        per_ref = lax.optimization_barrier(jnp.sum(weights.reshape(block_room, NSHIFT, R_DEV), axis=1))
        ctf_rows = ctf_rows_all[row_ids]
        weight_block = jnp.dot(per_ref.T, ctf_rows * ctf_rows, precision=lax.Precision.HIGHEST)
        gathered = jnp.dot(weights.astype(jnp.bfloat16).T, rows_data, preferred_element_type=jnp.float32)
        gathered = gathered.reshape(NSHIFT, R_DEV, 2 * pixel_count)
        g_real = gathered[..., :pixel_count]
        g_imag = gathered[..., pixel_count:]
        cos_b = grid_cos[:, None, :]
        sin_b = grid_sin[:, None, :]
        back_block = jnp.concatenate([lax.optimization_barrier(jnp.sum(cos_b * g_real + sin_b * g_imag, axis=0)), lax.optimization_barrier(jnp.sum(cos_b * g_imag - sin_b * g_real, axis=0))], axis=-1)
        return (back_block, weight_block)
    back_all, weight_all = lax.map(second_pass, (owners, ref_blocks))
    return (back_all.reshape(N_ORI * R_DEV, 2 * pixel_count), weight_all.reshape(N_ORI * R_DEV, pixel_count), evidence)
```

```python
import functools
import math

import jax
import jax.numpy as jnp
from jax import lax
from jax.experimental import pallas as pl
from jax.experimental.pallas import tpu as pltpu
from jax.sharding import PartitionSpec as P

PX = 128
PY = 65
BOX = 320
SIDE = 8
NSHIFT = 64
HALF = NSHIFT // 2
LANES = 128

two_pi = 2.0 * math.pi
pixel_count = PX * PY
steps = 5
chunk = pixel_count // steps


def frequencies():
    pixel = jnp.arange(pixel_count)
    row_ids = pixel // PY
    freq_x = jnp.where(row_ids < PX // 2, row_ids, row_ids - PX).astype(jnp.float32)
    freq_y = (pixel % PY).astype(jnp.float32)
    return freq_x, freq_y


def axis_table(freq, amounts):
    angle = two_pi * (amounts[:, None] * freq[None, :]) / BOX
    return jnp.cos(angle), jnp.sin(angle)


def outer_table(table_x, table_y):
    cx, sx = table_x
    cy, sy = table_y
    cosine = cx[:, None] * cy[None] - sx[:, None] * sy[None]
    sine = sx[:, None] * cy[None] + cx[:, None] * sy[None]
    count = cx.shape[0] * cy.shape[0]
    return cosine.reshape(count, -1), sine.reshape(count, -1)


def pick(table, ids):
    out = jnp.zeros((ids.shape[0], table.shape[1]), jnp.float32)
    for i in range(table.shape[0]):
        out = jnp.where(ids[:, None] == i, table[i][None, :], out)
    return out


def centered(particles, offsets, classes, ctf_table, freq_x, freq_y):
    class_picks = (classes[:, None] == jnp.arange(ctf_table.shape[0])[None, :]).astype(jnp.float32)
    ctf_rows = jnp.dot(class_picks, ctf_table, precision=lax.Precision.HIGHEST)
    amounts = jnp.arange(-2, 3).astype(jnp.float32)
    cx, sx = axis_table(freq_x, amounts)
    cy, sy = axis_table(freq_y, amounts)
    ox, oy = offsets[0] + 2, offsets[1] + 2
    cx, sx, cy, sy = pick(cx, ox), pick(sx, ox), pick(cy, oy), pick(sy, oy)
    cosine = cx * cy - sx * sy
    sine = sx * cy + cx * sy
    real_part = particles[:, :pixel_count].astype(jnp.float32)
    imag_part = particles[:, pixel_count:].astype(jnp.float32)
    return jnp.concatenate(
        [
            ctf_rows * (real_part * cosine + imag_part * sine),
            ctf_rows * (imag_part * cosine - real_part * sine),
        ],
        axis=-1,
    ).astype(jnp.bfloat16)


def score_kernel(rr_ref, ri_ref, mr_ref, mi_ref, cos_ref, sin_ref, out_ref, lse_ref, kern):
    step = pl.program_id(0)
    refs = mr_ref.shape[0]

    def lane_block(j, carry):
        lanes = pl.ds(pl.multiple_of(j * LANES, LANES), LANES)
        late = pl.ds(pl.multiple_of(chunk + j * LANES, LANES), LANES)
        re = mr_ref[:, lanes].astype(jnp.float32)
        im = mi_ref[:, lanes].astype(jnp.float32)
        for s in range(NSHIFT):
            c = cos_ref[s : s + 1, lanes]
            d = sin_ref[s : s + 1, lanes]
            kern[s * refs : (s + 1) * refs, lanes] = (c * re - d * im).astype(jnp.bfloat16)
            kern[s * refs : (s + 1) * refs, late] = (d * re + c * im).astype(jnp.bfloat16)
        return carry

    lax.fori_loop(0, chunk // LANES, lane_block, 0)

    @pl.when(step == 0)
    def _():
        out_ref[...] = jnp.zeros_like(out_ref)

    tile = 256

    def row_block(j, carry):
        rows = pl.ds(pl.multiple_of(j * tile, tile), tile)
        dims = (((1,), (1,)), ((), ()))
        part = lax.dot_general(
            kern[rows, :chunk], rr_ref[...], dims, preferred_element_type=jnp.float32
        )
        part += lax.dot_general(
            kern[rows, chunk:], ri_ref[...], dims, preferred_element_type=jnp.float32
        )
        out_ref[rows, :] += part
        return carry

    lax.fori_loop(0, NSHIFT * refs // tile, row_block, 0)

    @pl.when(step == steps - 1)
    def _():
        scores = out_ref[...] * (2.0 / math.sqrt(pixel_count))
        out_ref[...] = scores
        top = jnp.max(scores, axis=0, keepdims=True)
        total = jnp.sum(jnp.exp(scores - top), axis=0, keepdims=True)
        lse_ref[...] = top + jnp.log(total)


def score_call(rows, references, cosine, sine):
    n_rows, refs = rows.shape[0], references.shape[0]
    hyps = NSHIFT * refs
    return pl.pallas_call(
        score_kernel,
        grid=(steps,),
        in_specs=[
            pl.BlockSpec((n_rows, chunk), lambda i: (0, i)),
            pl.BlockSpec((n_rows, chunk), lambda i: (0, i + steps)),
            pl.BlockSpec((refs, chunk), lambda i: (0, i)),
            pl.BlockSpec((refs, chunk), lambda i: (0, i + steps)),
            pl.BlockSpec((NSHIFT, chunk), lambda i: (0, i)),
            pl.BlockSpec((NSHIFT, chunk), lambda i: (0, i)),
        ],
        out_specs=[
            pl.BlockSpec((hyps, n_rows), lambda i: (0, 0)),
            pl.BlockSpec((1, n_rows), lambda i: (0, 0)),
        ],
        out_shape=[
            jax.ShapeDtypeStruct((hyps, n_rows), jnp.float32),
            jax.ShapeDtypeStruct((1, n_rows), jnp.float32),
        ],
        scratch_shapes=[pltpu.VMEM((hyps, 2 * chunk), jnp.bfloat16)],
        compiler_params=pltpu.CompilerParams(vmem_limit_bytes=60 * 2**20),
    )(rows, rows, references, references, cosine, sine)


def back_kernel(wp_ref, wm_ref, rr_ref, ri_ref, cos_ref, sin_ref, hc_ref, hs_ref, re_ref, im_ref):
    refs = re_ref.shape[0]

    def lane_block(j, carry):
        lanes = pl.ds(pl.multiple_of(j * LANES, LANES), LANES)
        panel = jnp.concatenate([rr_ref[:, lanes], ri_ref[:, lanes]], axis=1)
        even = jnp.dot(wp_ref[...], panel, preferred_element_type=jnp.float32)
        odd = jnp.dot(wm_ref[...], panel, preferred_element_type=jnp.float32)
        re = jnp.zeros((refs, LANES), jnp.float32)
        im = jnp.zeros((refs, LANES), jnp.float32)
        for s in range(HALF):
            c = cos_ref[s : s + 1, lanes]
            d = sin_ref[s : s + 1, lanes]
            e = even[s * refs : (s + 1) * refs]
            o = odd[s * refs : (s + 1) * refs]
            re += c * e[:, :LANES] + d * o[:, LANES:]
            im += c * e[:, LANES:] - d * o[:, :LANES]
        hc = hc_ref[:, lanes]
        hs = hs_ref[:, lanes]
        re_ref[:, lanes] = hc * re - hs * im
        im_ref[:, lanes] = hc * im + hs * re
        return carry

    lax.fori_loop(0, chunk // LANES, lane_block, 0)


def back_call(w_even, w_odd, rows, cosine, sine, half_cos, half_sin, refs):
    n_rows = rows.shape[0]
    whole = pl.BlockSpec(w_even.shape, lambda i: (0, 0))
    part = lambda count: pl.BlockSpec((count, chunk), lambda i: (0, i))
    return pl.pallas_call(
        back_kernel,
        grid=(steps,),
        in_specs=[
            whole,
            whole,
            part(n_rows),
            pl.BlockSpec((n_rows, chunk), lambda i: (0, i + steps)),
            part(HALF),
            part(HALF),
            part(1),
            part(1),
        ],
        out_specs=[part(refs), part(refs)],
        out_shape=[jax.ShapeDtypeStruct((refs, pixel_count), jnp.float32)] * 2,
        compiler_params=pltpu.CompilerParams(vmem_limit_bytes=60 * 2**20),
        cost_estimate=pl.CostEstimate(
            flops=4 * HALF * refs * n_rows * 2 * pixel_count,
            bytes_accessed=4 * n_rows * pixel_count,
            transcendentals=0,
        ),
    )(w_even, w_odd, rows, rows, cosine, sine, half_cos, half_sin)


def per_device(particles, priors, offsets, classes, ctf_table, references):
    n_ori = lax.axis_size("ori")
    n_grp = lax.axis_size("grp")
    me = lax.axis_index("ori")
    part_count = priors.shape[0]
    refs = references.shape[0]
    n_classes = ctf_table.shape[0]
    freq_x, freq_y = frequencies()
    shifted = centered(particles, offsets, classes, ctf_table, freq_x, freq_y)
    rows = lax.all_gather(shifted, "ori", axis=0, tiled=True)
    facts = lax.all_gather(
        jnp.concatenate([priors, classes[:, None]], axis=1).T, "ori", axis=1, tiled=True
    )
    first, second, row_class = facts[0], facts[1], facts[2]

    whole_steps = jnp.arange(SIDE).astype(jnp.float32) - SIDE // 2
    cosine, sine = outer_table(axis_table(freq_x, whole_steps), axis_table(freq_y, whole_steps))
    near = whole_steps + 0.5
    near_cos, near_sin = outer_table(
        axis_table(freq_x, near[: SIDE // 2]), axis_table(freq_y, near)
    )
    half_angle = (0.5 * two_pi / BOX) * (freq_x + freq_y)[None, :]
    half_cos, half_sin = jnp.cos(half_angle), jnp.sin(half_angle)

    scores, lse = score_call(rows, references, cosine, sine)
    all_lse = lax.all_gather(lse[0], "ori", axis=0, tiled=False)
    owners = jnp.arange(n_ori)[:, None]
    named = (first[None, :] == owners) | (second[None, :] == owners)
    kept = jnp.where(named, all_lse, -jnp.inf)
    top = jnp.max(kept, axis=0)
    evidence = top + jnp.log(jnp.sum(jnp.exp(kept - top[None, :]), axis=0))

    mine = (first == me) | (second == me)
    weights = jnp.where(mine[None, :], jnp.exp(scores - evidence[None, :]), 0.0)
    weights = weights.reshape(NSHIFT, refs, -1)
    per_ref = jnp.sum(weights, axis=0)
    ahead = weights[:HALF]
    behind = weights[HALF:][::-1]
    w_even = (ahead + behind).astype(jnp.bfloat16).reshape(HALF * refs, -1)
    w_odd = (ahead - behind).astype(jnp.bfloat16).reshape(HALF * refs, -1)

    class_picks = (row_class[:, None] == jnp.arange(n_classes)[None, :]).astype(jnp.float32)
    by_class = jnp.dot(per_ref, class_picks, precision=lax.Precision.HIGHEST)
    by_class = lax.psum(by_class, "grp")
    width = pixel_count // n_grp
    table_part = lax.dynamic_slice_in_dim(ctf_table, lax.axis_index("grp") * width, width, 1)
    weight_part = jnp.dot(by_class, table_part * table_part, precision=lax.Precision.HIGHEST)

    back_re, back_im = back_call(
        w_even, w_odd, rows, near_cos, near_sin, half_cos, half_sin, refs
    )
    pieces = [
        jnp.transpose(x.reshape(refs, n_grp // 2, -1), (1, 0, 2)) for x in (back_re, back_im)
    ]
    back_part = lax.psum_scatter(
        jnp.concatenate(pieces, axis=0), "grp", scatter_dimension=0, tiled=False
    )
    own = lax.dynamic_slice_in_dim(evidence, me * part_count, part_count, 0)
    return (back_part, weight_part, own)


def solution(mesh):
    placed = (
        P(("grp", "ori"), None),
        P(("grp", "ori"), None),
        P(None, ("grp", "ori")),
        P(("grp", "ori")),
        P(),
        P("ori", None),
    )
    return jax.shard_map(
        per_device,
        mesh=mesh,
        in_specs=placed,
        out_specs=(P("ori", "grp"), P("ori", "grp"), P(("grp", "ori"))),
        check_vma=False,
    )
```

```python
import functools
import math

import jax
import jax.numpy as jnp
from jax import lax
from jax.experimental import pallas as pl
from jax.experimental.pallas import tpu as pltpu
from jax.sharding import PartitionSpec as P

PX = 128
PY = 65
BOX = 320
SIDE = 8
NSHIFT = 64
HALF = NSHIFT // 2
LANES = 128

two_pi = 2.0 * math.pi
pixel_count = PX * PY
steps = 5
chunk = pixel_count // steps


def frequencies():
    pixel = jnp.arange(pixel_count)
    row_ids = pixel // PY
    freq_x = jnp.where(row_ids < PX // 2, row_ids, row_ids - PX).astype(jnp.float32)
    freq_y = (pixel % PY).astype(jnp.float32)
    return freq_x, freq_y


def axis_table(freq, amounts):
    angle = two_pi * (amounts[:, None] * freq[None, :]) / BOX
    return jnp.cos(angle), jnp.sin(angle)


def outer_table(table_x, table_y):
    cx, sx = table_x
    cy, sy = table_y
    cosine = cx[:, None] * cy[None] - sx[:, None] * sy[None]
    sine = sx[:, None] * cy[None] + cx[:, None] * sy[None]
    count = cx.shape[0] * cy.shape[0]
    return cosine.reshape(count, -1), sine.reshape(count, -1)


def pick(table, ids):
    out = jnp.zeros((ids.shape[0], table.shape[1]), jnp.float32)
    for i in range(table.shape[0]):
        out = jnp.where(ids[:, None] == i, table[i][None, :], out)
    return out


def centered(particles, offsets, classes, ctf_table, freq_x, freq_y):
    class_picks = (classes[:, None] == jnp.arange(ctf_table.shape[0])[None, :]).astype(jnp.float32)
    ctf_rows = jnp.dot(class_picks, ctf_table, precision=lax.Precision.HIGHEST)
    amounts = jnp.arange(-2, 3).astype(jnp.float32)
    cx, sx = axis_table(freq_x, amounts)
    cy, sy = axis_table(freq_y, amounts)
    ox, oy = offsets[0] + 2, offsets[1] + 2
    cx, sx, cy, sy = pick(cx, ox), pick(sx, ox), pick(cy, oy), pick(sy, oy)
    cosine = cx * cy - sx * sy
    sine = sx * cy + cx * sy
    real_part = particles[:, :pixel_count].astype(jnp.float32)
    imag_part = particles[:, pixel_count:].astype(jnp.float32)
    return jnp.concatenate(
        [
            ctf_rows * (real_part * cosine + imag_part * sine),
            ctf_rows * (imag_part * cosine - real_part * sine),
        ],
        axis=-1,
    ).astype(jnp.bfloat16)


def score_kernel(rr_ref, ri_ref, mr_ref, mi_ref, cos_ref, sin_ref, out_ref, lse_ref, kern):
    step = pl.program_id(0)
    refs = mr_ref.shape[0]

    def lane_block(j, carry):
        lanes = pl.ds(pl.multiple_of(j * LANES, LANES), LANES)
        late = pl.ds(pl.multiple_of(chunk + j * LANES, LANES), LANES)
        re = mr_ref[:, lanes].astype(jnp.float32)
        im = mi_ref[:, lanes].astype(jnp.float32)
        for s in range(NSHIFT):
            c = cos_ref[s : s + 1, lanes]
            d = sin_ref[s : s + 1, lanes]
            kern[s * refs : (s + 1) * refs, lanes] = (c * re - d * im).astype(jnp.bfloat16)
            kern[s * refs : (s + 1) * refs, late] = (d * re + c * im).astype(jnp.bfloat16)
        return carry

    lax.fori_loop(0, chunk // LANES, lane_block, 0)

    @pl.when(step == 0)
    def _():
        out_ref[...] = jnp.zeros_like(out_ref)

    tile = 256

    def row_block(j, carry):
        rows = pl.ds(pl.multiple_of(j * tile, tile), tile)
        dims = (((1,), (1,)), ((), ()))
        part = lax.dot_general(
            kern[rows, :chunk], rr_ref[...], dims, preferred_element_type=jnp.float32
        )
        part += lax.dot_general(
            kern[rows, chunk:], ri_ref[...], dims, preferred_element_type=jnp.float32
        )
        out_ref[rows, :] += part
        return carry

    lax.fori_loop(0, NSHIFT * refs // tile, row_block, 0)

    @pl.when(step == steps - 1)
    def _():
        scores = out_ref[...] * (2.0 / math.sqrt(pixel_count))
        out_ref[...] = scores
        top = jnp.max(scores, axis=0, keepdims=True)
        total = jnp.sum(jnp.exp(scores - top), axis=0, keepdims=True)
        lse_ref[...] = top + jnp.log(total)


def score_call(rows, references, cosine, sine):
    n_rows, refs = rows.shape[0], references.shape[0]
    hyps = NSHIFT * refs
    return pl.pallas_call(
        score_kernel,
        grid=(steps,),
        in_specs=[
            pl.BlockSpec((n_rows, chunk), lambda i: (0, i)),
            pl.BlockSpec((n_rows, chunk), lambda i: (0, i + steps)),
            pl.BlockSpec((refs, chunk), lambda i: (0, i)),
            pl.BlockSpec((refs, chunk), lambda i: (0, i + steps)),
            pl.BlockSpec((NSHIFT, chunk), lambda i: (0, i)),
            pl.BlockSpec((NSHIFT, chunk), lambda i: (0, i)),
        ],
        out_specs=[
            pl.BlockSpec((hyps, n_rows), lambda i: (0, 0)),
            pl.BlockSpec((1, n_rows), lambda i: (0, 0)),
        ],
        out_shape=[
            jax.ShapeDtypeStruct((hyps, n_rows), jnp.float32),
            jax.ShapeDtypeStruct((1, n_rows), jnp.float32),
        ],
        scratch_shapes=[pltpu.VMEM((hyps, 2 * chunk), jnp.bfloat16)],
        compiler_params=pltpu.CompilerParams(vmem_limit_bytes=60 * 2**20),
    )(rows, rows, references, references, cosine, sine)


def back_kernel(wp_ref, wm_ref, rr_ref, ri_ref, cos_ref, sin_ref, hc_ref, hs_ref, re_ref, im_ref):
    refs = re_ref.shape[0]

    def lane_block(j, carry):
        lanes = pl.ds(pl.multiple_of(j * LANES, LANES), LANES)
        panel = jnp.concatenate([rr_ref[:, lanes], ri_ref[:, lanes]], axis=1)
        even = jnp.dot(wp_ref[...], panel, preferred_element_type=jnp.float32)
        odd = jnp.dot(wm_ref[...], panel, preferred_element_type=jnp.float32)
        re = jnp.zeros((refs, LANES), jnp.float32)
        im = jnp.zeros((refs, LANES), jnp.float32)
        for s in range(HALF):
            c = cos_ref[s : s + 1, lanes]
            d = sin_ref[s : s + 1, lanes]
            e = even[s * refs : (s + 1) * refs]
            o = odd[s * refs : (s + 1) * refs]
            re += c * e[:, :LANES] + d * o[:, LANES:]
            im += c * e[:, LANES:] - d * o[:, :LANES]
        hc = hc_ref[:, lanes]
        hs = hs_ref[:, lanes]
        re_ref[:, lanes] = hc * re - hs * im
        im_ref[:, lanes] = hc * im + hs * re
        return carry

    lax.fori_loop(0, chunk // LANES, lane_block, 0)


def back_call(w_even, w_odd, rows, cosine, sine, half_cos, half_sin, refs):
    n_rows = rows.shape[0]
    whole = pl.BlockSpec(w_even.shape, lambda i: (0, 0))
    part = lambda count: pl.BlockSpec((count, chunk), lambda i: (0, i))
    return pl.pallas_call(
        back_kernel,
        grid=(steps,),
        in_specs=[
            whole,
            whole,
            part(n_rows),
            pl.BlockSpec((n_rows, chunk), lambda i: (0, i + steps)),
            part(HALF),
            part(HALF),
            part(1),
            part(1),
        ],
        out_specs=[part(refs), part(refs)],
        out_shape=[jax.ShapeDtypeStruct((refs, pixel_count), jnp.float32)] * 2,
        compiler_params=pltpu.CompilerParams(vmem_limit_bytes=60 * 2**20),
        cost_estimate=pl.CostEstimate(
            flops=4 * HALF * refs * n_rows * 2 * pixel_count,
            bytes_accessed=4 * n_rows * pixel_count,
            transcendentals=0,
        ),
    )(w_even, w_odd, rows, rows, cosine, sine, half_cos, half_sin)


def per_device_plain(particles, priors, offsets, classes, ctf_table, references):
    n_ori = lax.axis_size("ori")
    n_grp = lax.axis_size("grp")
    me = lax.axis_index("ori")
    part_count = priors.shape[0]
    refs = references.shape[0]
    n_classes = ctf_table.shape[0]
    freq_x, freq_y = frequencies()
    shifted = centered(particles, offsets, classes, ctf_table, freq_x, freq_y)
    rows = lax.all_gather(shifted, "ori", axis=0, tiled=True)
    facts = lax.all_gather(
        jnp.concatenate([priors, classes[:, None]], axis=1).T, "ori", axis=1, tiled=True
    )
    first, second, row_class = facts[0], facts[1], facts[2]

    whole_steps = jnp.arange(SIDE).astype(jnp.float32) - SIDE // 2
    cosine, sine = outer_table(axis_table(freq_x, whole_steps), axis_table(freq_y, whole_steps))
    near = whole_steps + 0.5
    near_cos, near_sin = outer_table(
        axis_table(freq_x, near[: SIDE // 2]), axis_table(freq_y, near)
    )
    half_angle = (0.5 * two_pi / BOX) * (freq_x + freq_y)[None, :]
    half_cos, half_sin = jnp.cos(half_angle), jnp.sin(half_angle)

    scores, lse = score_call(rows, references, cosine, sine)
    all_lse = lax.all_gather(lse[0], "ori", axis=0, tiled=False)
    owners = jnp.arange(n_ori)[:, None]
    named = (first[None, :] == owners) | (second[None, :] == owners)
    kept = jnp.where(named, all_lse, -jnp.inf)
    top = jnp.max(kept, axis=0)
    evidence = top + jnp.log(jnp.sum(jnp.exp(kept - top[None, :]), axis=0))

    mine = (first == me) | (second == me)
    weights = jnp.where(mine[None, :], jnp.exp(scores - evidence[None, :]), 0.0)
    weights = weights.reshape(NSHIFT, refs, -1)
    per_ref = jnp.sum(weights, axis=0)
    ahead = weights[:HALF]
    behind = weights[HALF:][::-1]
    w_even = (ahead + behind).astype(jnp.bfloat16).reshape(HALF * refs, -1)
    w_odd = (ahead - behind).astype(jnp.bfloat16).reshape(HALF * refs, -1)

    class_picks = (row_class[:, None] == jnp.arange(n_classes)[None, :]).astype(jnp.float32)
    by_class = jnp.dot(per_ref, class_picks, precision=lax.Precision.HIGHEST)
    by_class = lax.psum(by_class, "grp")
    width = pixel_count // n_grp
    table_part = lax.dynamic_slice_in_dim(ctf_table, lax.axis_index("grp") * width, width, 1)
    weight_part = jnp.dot(by_class, table_part * table_part, precision=lax.Precision.HIGHEST)

    back_re, back_im = back_call(
        w_even, w_odd, rows, near_cos, near_sin, half_cos, half_sin, refs
    )
    pieces = [
        jnp.transpose(x.reshape(refs, n_grp // 2, -1), (1, 0, 2)) for x in (back_re, back_im)
    ]
    back_part = lax.psum_scatter(
        jnp.concatenate(pieces, axis=0), "grp", scatter_dimension=0, tiled=False
    )
    own = lax.dynamic_slice_in_dim(evidence, me * part_count, part_count, 0)
    return (back_part, weight_part, own)


N_CHUNK = 13
CHUNK_PX = pixel_count // N_CHUNK
CHUNK_BLOCKS = CHUNK_PX // LANES
PIECES = 11
PIECE_BLOCKS = 3
MESH = pl.DeviceIdType.MESH


def square(z):
    c, s = z
    return c * c - s * s, 2.0 * c * s


def times(z, y):
    return z[0] * y[0] - z[1] * y[1], z[0] * y[1] + z[1] * y[0]


def step_table(half):
    one = square(half)
    two = square(one)
    four = square(two)
    k = lax.broadcasted_iota(jnp.int32, (SIDE, LANES), 0)
    out = (jnp.broadcast_to(four[0], (SIDE, LANES)), jnp.broadcast_to(-four[1], (SIDE, LANES)))
    for bit, z in ((1, one), (2, two), (4, four)):
        on = (k // bit) % 2 == 1
        out = times(out, (jnp.where(on, z[0], 1.0), jnp.where(on, z[1], 0.0)))
    return out


def offset_phase(half, ids):
    one = square(half)
    two = square(one)
    size = jnp.abs(ids)
    c = jnp.where(size == 0, 1.0, jnp.where(size == 1, one[0], two[0]))
    s = jnp.where(size == 0, 0.0, jnp.where(size == 1, one[1], two[1]))
    return c, jnp.where(ids < 0, -s, s)


def fused_kernel(
    n_ori,
    n_grp,
    prt,
    info,
    facts,
    base,
    ctf,
    mref,
    back_out,
    class_out,
    ev_out,
    rows,
    kern,
    scores,
    wp,
    wm,
    tab_c,
    tab_s,
    fbuf,
    lbuf,
    cbuf,
    part,
    rbuf,
    row_send,
    row_recv,
    f_send,
    f_recv,
    l_send,
    l_recv,
    c_send,
    c_recv,
    b_send,
    b_recv,
):
    g = lax.axis_index("grp")
    me = lax.axis_index("ori")
    per = prt.shape[0]
    refs = mref.shape[0]
    core = lax.rem(me, 2)
    px = lax.rem(me // 2, 2)
    py = me // 4
    dx = 2 * (1 - 2 * px)
    dy = 4 * (1 - 2 * py)
    sib = me + 1 - 2 * core
    xn, yn, diag = me + dx, me + dy, me + dx + dy

    barrier = pltpu.get_barrier_semaphore()
    for k in range(1, n_ori):
        pl.semaphore_signal(
            barrier, inc=1, device_id=(g, lax.rem(me + k, n_ori)), device_id_type=MESH
        )
    for k in range(1, n_grp):
        pl.semaphore_signal(
            barrier, inc=1, device_id=(lax.rem(g + k, n_grp), me), device_id_type=MESH
        )

    def halves(lanes):
        return (
            (base[0:1, lanes], base[1:2, lanes]),
            (base[2:3, lanes], base[3:4, lanes]),
        )

    cls = info[:, 0:1]
    ox = info[:, 1:2]
    oy = info[:, 2:3]

    def center_block(j, carry):
        c = j // CHUNK_BLOCKS
        off = lax.rem(j, CHUNK_BLOCKS) * LANES
        lanes = pl.ds(pl.multiple_of(j * LANES, LANES), LANES)
        late = pl.ds(pl.multiple_of(pixel_count + j * LANES, LANES), LANES)
        hx, hy = halves(lanes)
        cosine, sine = times(offset_phase(hx, ox), offset_phase(hy, oy))
        amp = jnp.zeros((per, LANES), jnp.float32)
        for i in range(ctf.shape[0]):
            amp = jnp.where(cls == i, ctf[i : i + 1, lanes], amp)
        re = prt[:, lanes].astype(jnp.float32)
        im = prt[:, late].astype(jnp.float32)
        mine = pl.ds(pl.multiple_of(me * per, per), per)
        rows[c, mine, pl.ds(pl.multiple_of(off, LANES), LANES)] = (
            amp * (re * cosine + im * sine)
        ).astype(jnp.bfloat16)
        rows[c, mine, pl.ds(pl.multiple_of(CHUNK_PX + off, LANES), LANES)] = (
            amp * (im * cosine - re * sine)
        ).astype(jnp.bfloat16)
        return carry

    lax.fori_loop(0, N_CHUNK * CHUNK_BLOCKS, center_block, 0)

    pl.semaphore_wait(barrier, n_ori - 1 + n_grp - 1)

    half_rows = per // 2
    plan = (
        (me, 0, per, xn),
        (me, 0, per, yn),
        (me, 0, per, sib),
        (xn, 0, half_rows, yn),
        (yn, half_rows, half_rows, xn),
        (xn, 0, per, sib),
        (yn, 0, per, sib),
        (diag, 0, half_rows, sib),
        (diag, half_rows, half_rows, sib),
    )

    def row_copy(kind, c):
        owner, first, count, target = plan[kind]
        piece = rows.at[c, pl.ds(pl.multiple_of(owner * per + first, half_rows), count)]
        return pltpu.make_async_remote_copy(
            src_ref=piece,
            dst_ref=piece,
            send_sem=row_send.at[kind, c],
            recv_sem=row_recv.at[kind, c],
            device_id=(g, target),
            device_id_type=MESH,
        )

    def fact_copy(k):
        return pltpu.make_async_remote_copy(
            src_ref=facts,
            dst_ref=fbuf.at[k],
            send_sem=f_send.at[k],
            recv_sem=f_recv.at[k],
            device_id=(g, lax.rem(me + k, n_ori)),
            device_id_type=MESH,
        )

    def lse_copy(k):
        return pltpu.make_async_remote_copy(
            src_ref=lbuf.at[me],
            dst_ref=lbuf.at[me],
            send_sem=l_send.at[k],
            recv_sem=l_recv.at[k],
            device_id=(g, lax.rem(me + k, n_ori)),
            device_id_type=MESH,
        )

    def class_copy(k):
        return pltpu.make_async_remote_copy(
            src_ref=cbuf.at[0],
            dst_ref=cbuf.at[k],
            send_sem=c_send.at[k],
            recv_sem=c_recv.at[k],
            device_id=(lax.rem(g + k, n_grp), me),
            device_id_type=MESH,
        )

    def back_copy(k, i):
        to = lax.rem(g + k, n_grp)
        return pltpu.make_async_remote_copy(
            src_ref=part.at[i, to],
            dst_ref=rbuf.at[k, i],
            send_sem=b_send.at[k, i],
            recv_sem=b_recv.at[k, i],
            device_id=(to, me),
            device_id_type=MESH,
        )

    for c in range(2):
        for kind in range(3):
            row_copy(kind, c).start()
    for k in range(1, n_ori):
        fact_copy(k).start()

    scores[...] = jnp.zeros_like(scores)

    def make_kernels(c):
        def lane_block(j, carry):
            at = c * CHUNK_PX + j * LANES
            lanes = pl.ds(pl.multiple_of(at, LANES), LANES)
            late = pl.ds(pl.multiple_of(pixel_count + at, LANES), LANES)
            near = pl.ds(pl.multiple_of(j * LANES, LANES), LANES)
            far = pl.ds(pl.multiple_of(CHUNK_PX + j * LANES, LANES), LANES)
            hx, hy = halves(lanes)
            cx, sx = step_table(hx)
            cy, sy = step_table(hy)
            for a in range(SIDE):
                tc, ts = times((cx[a : a + 1], sx[a : a + 1]), (cy, sy))
                tab_c[a * SIDE : (a + 1) * SIDE] = tc
                tab_s[a * SIDE : (a + 1) * SIDE] = ts
            re = mref[:, lanes].astype(jnp.float32)
            im = mref[:, late].astype(jnp.float32)
            for s in range(NSHIFT):
                p = tab_c[s : s + 1]
                q = tab_s[s : s + 1]
                kern[s * refs : (s + 1) * refs, near] = (p * re - q * im).astype(jnp.bfloat16)
                kern[s * refs : (s + 1) * refs, far] = (q * re + p * im).astype(jnp.bfloat16)
            return carry

        lax.fori_loop(0, CHUNK_BLOCKS, lane_block, 0)

    tile = 256

    def add_scores(c):
        def row_block(j, carry):
            at = pl.ds(pl.multiple_of(j * tile, tile), tile)
            scores[at, :] += lax.dot_general(
                kern[at, :],
                rows[c],
                (((1,), (1,)), ((), ())),
                preferred_element_type=jnp.float32,
            )
            return carry

        lax.fori_loop(0, NSHIFT * refs // tile, row_block, 0)

    def gather_step(t, carry):
        @pl.when(t + 2 < N_CHUNK)
        def _():
            for kind in range(3):
                row_copy(kind, t + 2).start()

        @pl.when(t < N_CHUNK)
        def _():
            row_copy(0, t).wait_recv()
            row_copy(3, t).start()
            row_copy(5, t).start()
            row_copy(1, t).wait_recv()
            row_copy(4, t).start()
            row_copy(6, t).start()

        @pl.when((t >= 1) & (t < N_CHUNK + 1))
        def _():
            row_copy(3, t - 1).wait_recv()
            row_copy(7, t - 1).start()
            row_copy(4, t - 1).wait_recv()
            row_copy(8, t - 1).start()

        @pl.when(t >= 2)
        def _():
            c = t - 2
            make_kernels(c)
            for kind in (2, 5, 6, 7, 8):
                row_copy(kind, c).wait_recv()
            add_scores(c)

        return carry

    lax.fori_loop(0, N_CHUNK + 2, gather_step, 0)

    scale = 2.0 / math.sqrt(pixel_count)
    top = jnp.max(scores[...], axis=0, keepdims=True) * scale
    total = jnp.sum(jnp.exp(scores[...] * scale - top), axis=0, keepdims=True)
    lbuf[me] = top + jnp.log(total)
    for k in range(1, n_ori):
        lse_copy(k).start()

    seen = facts[...]
    for k in range(1, n_ori):
        fact_copy(k).wait_recv()
        seen = seen + fbuf[k]
    first, second, row_class = seen[0:1], seen[1:2], seen[2:3]
    mine = (first == me) | (second == me)

    for k in range(1, n_ori):
        lse_copy(k).wait_recv()
    peak = jnp.full(first.shape, -jnp.inf, jnp.float32)
    for o in range(n_ori):
        peak = jnp.where((first == o) | (second == o), jnp.maximum(peak, lbuf[o]), peak)
    mass = jnp.zeros(first.shape, jnp.float32)
    for o in range(n_ori):
        mass += jnp.where((first == o) | (second == o), jnp.exp(lbuf[o] - peak), 0.0)
    evidence = peak + jnp.log(mass)
    ev_out[...] = evidence

    def weigh(s, per_ref):
        near = pl.ds(pl.multiple_of(s * refs, refs), refs)
        far = pl.ds(pl.multiple_of((NSHIFT - 1 - s) * refs, refs), refs)
        ahead = jnp.where(mine, jnp.exp(scores[near, :] * scale - evidence), 0.0)
        behind = jnp.where(mine, jnp.exp(scores[far, :] * scale - evidence), 0.0)
        both = ahead + behind
        wp[near, :] = both.astype(jnp.bfloat16)
        wm[near, :] = (ahead - behind).astype(jnp.bfloat16)
        return per_ref + both

    per_ref = lax.fori_loop(
        0, HALF, weigh, jnp.zeros((refs, scores.shape[1]), jnp.float32), unroll=4
    )
    class_rows = lax.broadcasted_iota(jnp.int32, (LANES, scores.shape[1]), 0)
    picks = (class_rows == row_class).astype(jnp.float32)
    cbuf[0] = lax.dot_general(
        per_ref,
        picks,
        (((1,), (1,)), ((), ())),
        precision=lax.Precision.HIGHEST,
        preferred_element_type=jnp.float32,
    )

    def back_block(i, b, h):
        j = h * (n_grp * 8) + i * PIECE_BLOCKS + b
        c = j // CHUNK_BLOCKS
        off = lax.rem(j, CHUNK_BLOCKS) * LANES
        lanes = pl.ds(pl.multiple_of(j * LANES, LANES), LANES)
        hx, hy = halves(lanes)
        cx, sx = times(step_table(hx), hx)
        cy, sy = times(step_table(hy), hy)
        for a in range(SIDE // 2):
            tc, ts = times((cx[a : a + 1], sx[a : a + 1]), (cy, sy))
            tab_c[a * SIDE : (a + 1) * SIDE] = tc
            tab_s[a * SIDE : (a + 1) * SIDE] = ts
        panel = jnp.concatenate(
            [
                rows[c, :, pl.ds(pl.multiple_of(off, LANES), LANES)],
                rows[c, :, pl.ds(pl.multiple_of(CHUNK_PX + off, LANES), LANES)],
            ],
            axis=1,
        )
        even = jnp.dot(wp[...], panel, preferred_element_type=jnp.float32)
        odd = jnp.dot(wm[...], panel, preferred_element_type=jnp.float32)
        re = jnp.zeros((refs, LANES), jnp.float32)
        im = jnp.zeros((refs, LANES), jnp.float32)
        for s in range(HALF):
            p = tab_c[s : s + 1]
            q = tab_s[s : s + 1]
            e = even[s * refs : (s + 1) * refs]
            o = odd[s * refs : (s + 1) * refs]
            re += p * e[:, :LANES] + q * o[:, LANES:]
            im += p * e[:, LANES:] - q * o[:, :LANES]
        hc, hs = times(hx, hy)
        at = pl.ds(pl.multiple_of(b * LANES, LANES), LANES)
        part[i, h, :, at] = hc * re - hs * im
        part[i, 2 + h, :, at] = hc * im + hs * re

    def back_piece(i, carry):
        def one(n, inner):
            back_block(i, n // 2, lax.rem(n, 2))
            return inner

        lax.fori_loop(0, 2 * PIECE_BLOCKS, one, 0)

        @pl.when(i == 0)
        def _():
            for k in range(1, n_grp):
                class_copy(k).start()

        @pl.when(i > 0)
        def _():
            for k in range(1, n_grp):
                back_copy(k, i - 1).start()

        return carry

    lax.fori_loop(0, PIECES, back_piece, 0)
    for k in range(1, n_grp):
        back_copy(k, PIECES - 1).start()

    for k in range(1, n_grp):
        class_copy(k).wait_recv()
    class_out[...] = (cbuf[0] + cbuf[1]) + (cbuf[2] + cbuf[3])

    wide = PIECE_BLOCKS * LANES

    def finish(i, carry):
        for k in range(1, n_grp):
            back_copy(k, i).wait_recv()
        at = pl.ds(pl.multiple_of(i * wide, LANES), wide)
        back_out[:, at] = (part[i, g] + rbuf[1, i]) + (rbuf[2, i] + rbuf[3, i])
        for k in range(1, n_grp):
            back_copy(k, i).wait_send()
        return carry

    lax.fori_loop(0, PIECES, finish, 0)

    def drain(c, carry):
        for kind in range(9):
            row_copy(kind, c).wait_send()
        return carry

    lax.fori_loop(0, N_CHUNK, drain, 0)
    for k in range(1, n_ori):
        fact_copy(k).wait_send()
        lse_copy(k).wait_send()
    for k in range(1, n_grp):
        class_copy(k).wait_send()


def per_device_fused(particles, priors, offsets, classes, ctf_table, references):
    n_ori = lax.axis_size("ori")
    n_grp = lax.axis_size("grp")
    me = lax.axis_index("ori")
    g = lax.axis_index("grp")
    per = priors.shape[0]
    refs = references.shape[0]
    n_rows = n_ori * per
    hyps = NSHIFT * refs
    freq_x, freq_y = frequencies()
    ax, ay = freq_x * (0.5 * two_pi / BOX), freq_y * (0.5 * two_pi / BOX)
    base = jnp.stack([jnp.cos(ax), jnp.sin(ax), jnp.cos(ay), jnp.sin(ay)])
    info = jnp.stack([classes, offsets[0], offsets[1]], axis=1)
    listed = jnp.stack([priors[:, 0], priors[:, 1], classes])
    listed = jnp.pad(listed, ((0, 5), (0, 0)))
    placed = jnp.tile(listed, (1, n_ori))
    facts = jnp.where(jnp.arange(n_rows)[None, :] // per == me, placed, 0)
    wide = PIECES * PIECE_BLOCKS * LANES
    vmem = pl.BlockSpec(memory_space=pltpu.VMEM)
    sems = pltpu.SemaphoreType.DMA
    back, by_class, evidence = pl.pallas_call(
        functools.partial(fused_kernel, n_ori, n_grp),
        out_shape=[
            jax.ShapeDtypeStruct((refs, wide), jnp.float32),
            jax.ShapeDtypeStruct((refs, LANES), jnp.float32),
            jax.ShapeDtypeStruct((1, n_rows), jnp.float32),
        ],
        in_specs=[vmem] * 6,
        out_specs=[vmem] * 3,
        scratch_shapes=[
            pltpu.VMEM((N_CHUNK, n_rows, 2 * CHUNK_PX), jnp.bfloat16),
            pltpu.VMEM((hyps, 2 * CHUNK_PX), jnp.bfloat16),
            pltpu.VMEM((hyps, n_rows), jnp.float32),
            pltpu.VMEM((hyps // 2, n_rows), jnp.bfloat16),
            pltpu.VMEM((hyps // 2, n_rows), jnp.bfloat16),
            pltpu.VMEM((NSHIFT, LANES), jnp.float32),
            pltpu.VMEM((NSHIFT, LANES), jnp.float32),
            pltpu.VMEM((n_ori, 8, n_rows), jnp.int32),
            pltpu.VMEM((n_ori, 1, n_rows), jnp.float32),
            pltpu.VMEM((n_grp, refs, LANES), jnp.float32),
            pltpu.VMEM((PIECES, n_grp, refs, PIECE_BLOCKS * LANES), jnp.float32),
            pltpu.VMEM((n_grp, PIECES, refs, PIECE_BLOCKS * LANES), jnp.float32),
            sems((9, N_CHUNK)),
            sems((9, N_CHUNK)),
            sems((n_ori,)),
            sems((n_ori,)),
            sems((n_ori,)),
            sems((n_ori,)),
            sems((n_grp,)),
            sems((n_grp,)),
            sems((n_grp, PIECES)),
            sems((n_grp, PIECES)),
        ],
        compiler_params=pltpu.CompilerParams(
            collective_id=0, has_side_effects=True, vmem_limit_bytes=56 * 2**20
        ),
    )(particles, info, facts, base, ctf_table, references)

    n_classes = ctf_table.shape[0]
    width = pixel_count // n_grp
    table_part = lax.dynamic_slice_in_dim(ctf_table, g * width, width, 1)
    weight_part = jnp.dot(
        by_class[:, :n_classes], table_part * table_part, precision=lax.Precision.HIGHEST
    )
    cols = 2 * width
    back_part = jnp.where(g % 2 == 0, back[:, :cols], back[:, wide - cols :])
    own = lax.dynamic_slice_in_dim(evidence[0], me * per, per, 0)
    return (back_part, weight_part, own)


def solution(mesh):
    small = mesh.shape["ori"] == 8 and mesh.shape["grp"] == 4
    per_device = per_device_fused if small else per_device_plain
    placed = (
        P(("grp", "ori"), None),
        P(("grp", "ori"), None),
        P(None, ("grp", "ori")),
        P(("grp", "ori")),
        P(),
        P("ori", None),
    )
    return jax.shard_map(
        per_device,
        mesh=mesh,
        in_specs=placed,
        out_specs=(P("ori", "grp"), P("ori", "grp"), P(("grp", "ori"))),
        check_vma=False,
    )
```

```python
import functools
import math

import jax
import jax.numpy as jnp
from jax import lax
from jax.experimental import pallas as pl
from jax.experimental.pallas import tpu as pltpu
from jax.sharding import PartitionSpec as P

PX = 128
PY = 65
BOX = 320
SIDE = 8
NSHIFT = 64
HALF = NSHIFT // 2
LANES = 128

two_pi = 2.0 * math.pi
pixel_count = PX * PY
steps = 5
chunk = pixel_count // steps


def frequencies():
    pixel = jnp.arange(pixel_count)
    row_ids = pixel // PY
    freq_x = jnp.where(row_ids < PX // 2, row_ids, row_ids - PX).astype(jnp.float32)
    freq_y = (pixel % PY).astype(jnp.float32)
    return freq_x, freq_y


def axis_table(freq, amounts):
    angle = two_pi * (amounts[:, None] * freq[None, :]) / BOX
    return jnp.cos(angle), jnp.sin(angle)


def outer_table(table_x, table_y):
    cx, sx = table_x
    cy, sy = table_y
    cosine = cx[:, None] * cy[None] - sx[:, None] * sy[None]
    sine = sx[:, None] * cy[None] + cx[:, None] * sy[None]
    count = cx.shape[0] * cy.shape[0]
    return cosine.reshape(count, -1), sine.reshape(count, -1)


def pick(table, ids):
    out = jnp.zeros((ids.shape[0], table.shape[1]), jnp.float32)
    for i in range(table.shape[0]):
        out = jnp.where(ids[:, None] == i, table[i][None, :], out)
    return out


def centered(particles, offsets, classes, ctf_table, freq_x, freq_y):
    class_picks = (classes[:, None] == jnp.arange(ctf_table.shape[0])[None, :]).astype(jnp.float32)
    ctf_rows = jnp.dot(class_picks, ctf_table, precision=lax.Precision.HIGHEST)
    amounts = jnp.arange(-2, 3).astype(jnp.float32)
    cx, sx = axis_table(freq_x, amounts)
    cy, sy = axis_table(freq_y, amounts)
    ox, oy = offsets[0] + 2, offsets[1] + 2
    cx, sx, cy, sy = pick(cx, ox), pick(sx, ox), pick(cy, oy), pick(sy, oy)
    cosine = cx * cy - sx * sy
    sine = sx * cy + cx * sy
    real_part = particles[:, :pixel_count].astype(jnp.float32)
    imag_part = particles[:, pixel_count:].astype(jnp.float32)
    return jnp.concatenate(
        [
            ctf_rows * (real_part * cosine + imag_part * sine),
            ctf_rows * (imag_part * cosine - real_part * sine),
        ],
        axis=-1,
    ).astype(jnp.bfloat16)


def score_kernel(rr_ref, ri_ref, mr_ref, mi_ref, cos_ref, sin_ref, out_ref, lse_ref, kern):
    step = pl.program_id(0)
    refs = mr_ref.shape[0]

    def lane_block(j, carry):
        lanes = pl.ds(pl.multiple_of(j * LANES, LANES), LANES)
        late = pl.ds(pl.multiple_of(chunk + j * LANES, LANES), LANES)
        re = mr_ref[:, lanes].astype(jnp.float32)
        im = mi_ref[:, lanes].astype(jnp.float32)
        for s in range(NSHIFT):
            c = cos_ref[s : s + 1, lanes]
            d = sin_ref[s : s + 1, lanes]
            kern[s * refs : (s + 1) * refs, lanes] = (c * re - d * im).astype(jnp.bfloat16)
            kern[s * refs : (s + 1) * refs, late] = (d * re + c * im).astype(jnp.bfloat16)
        return carry

    lax.fori_loop(0, chunk // LANES, lane_block, 0)

    @pl.when(step == 0)
    def _():
        out_ref[...] = jnp.zeros_like(out_ref)

    tile = 256

    def row_block(j, carry):
        rows = pl.ds(pl.multiple_of(j * tile, tile), tile)
        dims = (((1,), (1,)), ((), ()))
        part = lax.dot_general(
            kern[rows, :chunk], rr_ref[...], dims, preferred_element_type=jnp.float32
        )
        part += lax.dot_general(
            kern[rows, chunk:], ri_ref[...], dims, preferred_element_type=jnp.float32
        )
        out_ref[rows, :] += part
        return carry

    lax.fori_loop(0, NSHIFT * refs // tile, row_block, 0)

    @pl.when(step == steps - 1)
    def _():
        scores = out_ref[...] * (2.0 / math.sqrt(pixel_count))
        out_ref[...] = scores
        top = jnp.max(scores, axis=0, keepdims=True)
        total = jnp.sum(jnp.exp(scores - top), axis=0, keepdims=True)
        lse_ref[...] = top + jnp.log(total)


def score_call(rows, references, cosine, sine):
    n_rows, refs = rows.shape[0], references.shape[0]
    hyps = NSHIFT * refs
    return pl.pallas_call(
        score_kernel,
        grid=(steps,),
        in_specs=[
            pl.BlockSpec((n_rows, chunk), lambda i: (0, i)),
            pl.BlockSpec((n_rows, chunk), lambda i: (0, i + steps)),
            pl.BlockSpec((refs, chunk), lambda i: (0, i)),
            pl.BlockSpec((refs, chunk), lambda i: (0, i + steps)),
            pl.BlockSpec((NSHIFT, chunk), lambda i: (0, i)),
            pl.BlockSpec((NSHIFT, chunk), lambda i: (0, i)),
        ],
        out_specs=[
            pl.BlockSpec((hyps, n_rows), lambda i: (0, 0)),
            pl.BlockSpec((1, n_rows), lambda i: (0, 0)),
        ],
        out_shape=[
            jax.ShapeDtypeStruct((hyps, n_rows), jnp.float32),
            jax.ShapeDtypeStruct((1, n_rows), jnp.float32),
        ],
        scratch_shapes=[pltpu.VMEM((hyps, 2 * chunk), jnp.bfloat16)],
        compiler_params=pltpu.CompilerParams(vmem_limit_bytes=60 * 2**20),
    )(rows, rows, references, references, cosine, sine)


def back_kernel(wp_ref, wm_ref, rr_ref, ri_ref, cos_ref, sin_ref, hc_ref, hs_ref, re_ref, im_ref):
    refs = re_ref.shape[0]

    def lane_block(j, carry):
        lanes = pl.ds(pl.multiple_of(j * LANES, LANES), LANES)
        panel = jnp.concatenate([rr_ref[:, lanes], ri_ref[:, lanes]], axis=1)
        even = jnp.dot(wp_ref[...], panel, preferred_element_type=jnp.float32)
        odd = jnp.dot(wm_ref[...], panel, preferred_element_type=jnp.float32)
        re = jnp.zeros((refs, LANES), jnp.float32)
        im = jnp.zeros((refs, LANES), jnp.float32)
        for s in range(HALF):
            c = cos_ref[s : s + 1, lanes]
            d = sin_ref[s : s + 1, lanes]
            e = even[s * refs : (s + 1) * refs]
            o = odd[s * refs : (s + 1) * refs]
            re += c * e[:, :LANES] + d * o[:, LANES:]
            im += c * e[:, LANES:] - d * o[:, :LANES]
        hc = hc_ref[:, lanes]
        hs = hs_ref[:, lanes]
        re_ref[:, lanes] = hc * re - hs * im
        im_ref[:, lanes] = hc * im + hs * re
        return carry

    lax.fori_loop(0, chunk // LANES, lane_block, 0)


def back_call(w_even, w_odd, rows, cosine, sine, half_cos, half_sin, refs):
    n_rows = rows.shape[0]
    whole = pl.BlockSpec(w_even.shape, lambda i: (0, 0))
    part = lambda count: pl.BlockSpec((count, chunk), lambda i: (0, i))
    return pl.pallas_call(
        back_kernel,
        grid=(steps,),
        in_specs=[
            whole,
            whole,
            part(n_rows),
            pl.BlockSpec((n_rows, chunk), lambda i: (0, i + steps)),
            part(HALF),
            part(HALF),
            part(1),
            part(1),
        ],
        out_specs=[part(refs), part(refs)],
        out_shape=[jax.ShapeDtypeStruct((refs, pixel_count), jnp.float32)] * 2,
        compiler_params=pltpu.CompilerParams(vmem_limit_bytes=60 * 2**20),
        cost_estimate=pl.CostEstimate(
            flops=4 * HALF * refs * n_rows * 2 * pixel_count,
            bytes_accessed=4 * n_rows * pixel_count,
            transcendentals=0,
        ),
    )(w_even, w_odd, rows, rows, cosine, sine, half_cos, half_sin)


def per_device_plain(particles, priors, offsets, classes, ctf_table, references):
    n_ori = lax.axis_size("ori")
    n_grp = lax.axis_size("grp")
    me = lax.axis_index("ori")
    part_count = priors.shape[0]
    refs = references.shape[0]
    n_classes = ctf_table.shape[0]
    freq_x, freq_y = frequencies()
    shifted = centered(particles, offsets, classes, ctf_table, freq_x, freq_y)
    rows = lax.all_gather(shifted, "ori", axis=0, tiled=True)
    facts = lax.all_gather(
        jnp.concatenate([priors, classes[:, None]], axis=1).T, "ori", axis=1, tiled=True
    )
    first, second, row_class = facts[0], facts[1], facts[2]

    whole_steps = jnp.arange(SIDE).astype(jnp.float32) - SIDE // 2
    cosine, sine = outer_table(axis_table(freq_x, whole_steps), axis_table(freq_y, whole_steps))
    near = whole_steps + 0.5
    near_cos, near_sin = outer_table(
        axis_table(freq_x, near[: SIDE // 2]), axis_table(freq_y, near)
    )
    half_angle = (0.5 * two_pi / BOX) * (freq_x + freq_y)[None, :]
    half_cos, half_sin = jnp.cos(half_angle), jnp.sin(half_angle)

    scores, lse = score_call(rows, references, cosine, sine)
    all_lse = lax.all_gather(lse[0], "ori", axis=0, tiled=False)
    owners = jnp.arange(n_ori)[:, None]
    named = (first[None, :] == owners) | (second[None, :] == owners)
    kept = jnp.where(named, all_lse, -jnp.inf)
    top = jnp.max(kept, axis=0)
    evidence = top + jnp.log(jnp.sum(jnp.exp(kept - top[None, :]), axis=0))

    mine = (first == me) | (second == me)
    weights = jnp.where(mine[None, :], jnp.exp(scores - evidence[None, :]), 0.0)
    weights = weights.reshape(NSHIFT, refs, -1)
    per_ref = jnp.sum(weights, axis=0)
    ahead = weights[:HALF]
    behind = weights[HALF:][::-1]
    w_even = (ahead + behind).astype(jnp.bfloat16).reshape(HALF * refs, -1)
    w_odd = (ahead - behind).astype(jnp.bfloat16).reshape(HALF * refs, -1)

    class_picks = (row_class[:, None] == jnp.arange(n_classes)[None, :]).astype(jnp.float32)
    by_class = jnp.dot(per_ref, class_picks, precision=lax.Precision.HIGHEST)
    by_class = lax.psum(by_class, "grp")
    width = pixel_count // n_grp
    table_part = lax.dynamic_slice_in_dim(ctf_table, lax.axis_index("grp") * width, width, 1)
    weight_part = jnp.dot(by_class, table_part * table_part, precision=lax.Precision.HIGHEST)

    back_re, back_im = back_call(
        w_even, w_odd, rows, near_cos, near_sin, half_cos, half_sin, refs
    )
    pieces = [
        jnp.transpose(x.reshape(refs, n_grp // 2, -1), (1, 0, 2)) for x in (back_re, back_im)
    ]
    back_part = lax.psum_scatter(
        jnp.concatenate(pieces, axis=0), "grp", scatter_dimension=0, tiled=False
    )
    own = lax.dynamic_slice_in_dim(evidence, me * part_count, part_count, 0)
    return (back_part, weight_part, own)


N_CHUNK = 13
CHUNK_PX = pixel_count // N_CHUNK
CHUNK_BLOCKS = CHUNK_PX // LANES
PIECES = 11
PIECE_BLOCKS = 3
AHEAD = 4
MESH = pl.DeviceIdType.MESH


def small_phase(x):
    y = x * x
    c = jnp.ones_like(y)
    s = jnp.ones_like(y)
    for n in (5, 4, 3, 2, 1):
        c = 1.0 - y * c * (1.0 / ((2 * n - 1) * (2 * n)))
        s = 1.0 - y * s * (1.0 / ((2 * n) * (2 * n + 1)))
    return c, x * s


def square(z):
    c, s = z
    return c * c - s * s, 2.0 * c * s


def times(z, y):
    return z[0] * y[0] - z[1] * y[1], z[0] * y[1] + z[1] * y[0]


def step_table(half):
    one = square(half)
    two = square(one)
    four = square(two)
    k = lax.broadcasted_iota(jnp.int32, (SIDE, LANES), 0)
    out = (jnp.broadcast_to(four[0], (SIDE, LANES)), jnp.broadcast_to(-four[1], (SIDE, LANES)))
    for bit, z in ((1, one), (2, two), (4, four)):
        on = (k // bit) % 2 == 1
        out = times(out, (jnp.where(on, z[0], 1.0), jnp.where(on, z[1], 0.0)))
    return out


def offset_phase(half, ids):
    one = square(half)
    two = square(one)
    size = jnp.abs(ids)
    c = jnp.where(size == 0, 1.0, jnp.where(size == 1, one[0], two[0]))
    s = jnp.where(size == 0, 0.0, jnp.where(size == 1, one[1], two[1]))
    return c, jnp.where(ids < 0, -s, s)


def fused_kernel(
    n_ori,
    n_grp,
    prt,
    info,
    facts,
    ctf,
    mref,
    back_out,
    class_out,
    ev_out,
    rows,
    kern,
    scores,
    wp,
    wm,
    tab_c,
    tab_s,
    fbuf,
    lbuf,
    cbuf,
    part,
    sent,
    rbuf,
    base,
    row_send,
    row_recv,
    f_send,
    f_recv,
    l_send,
    l_recv,
    c_send,
    c_recv,
    b_send,
    b_recv,
):
    g = lax.axis_index("grp")
    me = lax.axis_index("ori")
    per = prt.shape[0]
    refs = mref.shape[0]
    core = lax.rem(me, 2)
    px = lax.rem(me // 2, 2)
    py = me // 4
    dx = 2 * (1 - 2 * px)
    dy = 4 * (1 - 2 * py)
    sib = me + 1 - 2 * core
    xn, yn, diag = me + dx, me + dy, me + dx + dy

    barrier = pltpu.get_barrier_semaphore()
    for k in range(1, n_ori):
        pl.semaphore_signal(
            barrier, inc=1, device_id=(g, lax.rem(me + k, n_ori)), device_id_type=MESH
        )
    for k in range(1, n_grp):
        pl.semaphore_signal(
            barrier, inc=1, device_id=(lax.rem(g + k, n_grp), me), device_id_type=MESH
        )

    pixel = lax.broadcasted_iota(jnp.int32, (1, pixel_count), 1).astype(jnp.float32)
    row = jnp.floor((pixel + 0.5) * (1.0 / PY))
    freq_y = pixel - row * PY
    freq_x = jnp.where(row < PX // 2, row, row - PX)
    for n, freq in enumerate((freq_x, freq_y)):
        cosine, sine = small_phase(freq * (0.5 * two_pi / BOX))
        base[2 * n : 2 * n + 1, :] = cosine
        base[2 * n + 1 : 2 * n + 2, :] = sine

    def halves(lanes):
        return (
            (base[0:1, lanes], base[1:2, lanes]),
            (base[2:3, lanes], base[3:4, lanes]),
        )

    cls = info[:, 0:1]
    ox = info[:, 1:2]
    oy = info[:, 2:3]

    def center_block(j, carry):
        c = j // CHUNK_BLOCKS
        off = lax.rem(j, CHUNK_BLOCKS) * LANES
        lanes = pl.ds(pl.multiple_of(j * LANES, LANES), LANES)
        late = pl.ds(pl.multiple_of(pixel_count + j * LANES, LANES), LANES)
        hx, hy = halves(lanes)
        cosine, sine = times(offset_phase(hx, ox), offset_phase(hy, oy))
        amp = jnp.zeros((per, LANES), jnp.float32)
        for i in range(ctf.shape[0]):
            amp = jnp.where(cls == i, ctf[i : i + 1, lanes], amp)
        re = prt[:, lanes].astype(jnp.float32)
        im = prt[:, late].astype(jnp.float32)
        mine = pl.ds(pl.multiple_of(me * per, per), per)
        rows[c, mine, pl.ds(pl.multiple_of(off, LANES), LANES)] = (
            amp * (re * cosine + im * sine)
        ).astype(jnp.bfloat16)
        rows[c, mine, pl.ds(pl.multiple_of(CHUNK_PX + off, LANES), LANES)] = (
            amp * (im * cosine - re * sine)
        ).astype(jnp.bfloat16)
        return carry

    def center_chunk(c):
        lax.fori_loop(c * CHUNK_BLOCKS, (c + 1) * CHUNK_BLOCKS, center_block, 0)

    for c in range(2):
        center_chunk(c)

    pl.semaphore_wait(barrier, n_ori - 1 + n_grp - 1)

    half_rows = per // 2
    plan = (
        (me, 0, per, xn),
        (me, 0, per, yn),
        (me, 0, per, sib),
        (xn, 0, half_rows, yn),
        (yn, half_rows, half_rows, xn),
        (xn, 0, per, sib),
        (yn, 0, per, sib),
        (diag, 0, half_rows, sib),
        (diag, half_rows, half_rows, sib),
    )

    def row_copy(kind, c):
        owner, first, count, target = plan[kind]
        piece = rows.at[c, pl.ds(pl.multiple_of(owner * per + first, half_rows), count)]
        return pltpu.make_async_remote_copy(
            src_ref=piece,
            dst_ref=piece,
            send_sem=row_send.at[kind, c],
            recv_sem=row_recv.at[kind, c],
            device_id=(g, target),
            device_id_type=MESH,
        )

    def fact_copy(k):
        return pltpu.make_async_remote_copy(
            src_ref=facts,
            dst_ref=fbuf.at[k],
            send_sem=f_send.at[k],
            recv_sem=f_recv.at[k],
            device_id=(g, lax.rem(me + k, n_ori)),
            device_id_type=MESH,
        )

    def lse_copy(k):
        return pltpu.make_async_remote_copy(
            src_ref=lbuf.at[me],
            dst_ref=lbuf.at[me],
            send_sem=l_send.at[k],
            recv_sem=l_recv.at[k],
            device_id=(g, lax.rem(me + k, n_ori)),
            device_id_type=MESH,
        )

    def class_copy(k):
        return pltpu.make_async_remote_copy(
            src_ref=cbuf.at[0],
            dst_ref=cbuf.at[k],
            send_sem=c_send.at[k],
            recv_sem=c_recv.at[k],
            device_id=(lax.rem(g + k, n_grp), me),
            device_id_type=MESH,
        )

    def back_copy(k, i):
        to = lax.rem(g + k, n_grp)
        return pltpu.make_async_remote_copy(
            src_ref=sent.at[i, to],
            dst_ref=rbuf.at[k, i],
            send_sem=b_send.at[k, i],
            recv_sem=b_recv.at[k, i],
            device_id=(to, me),
            device_id_type=MESH,
        )

    for kind in range(3):
        row_copy(kind, 0).start()
    for k in range(1, n_ori):
        fact_copy(k).start()

    def early(c, carry):
        center_chunk(c)
        for kind in range(3):
            row_copy(kind, c - 1).start()
        return carry

    lax.fori_loop(2, AHEAD + 1, early, 0)

    scores[...] = jnp.zeros_like(scores)

    def make_kernels(c):
        def lane_block(j, carry):
            at = c * CHUNK_PX + j * LANES
            lanes = pl.ds(pl.multiple_of(at, LANES), LANES)
            late = pl.ds(pl.multiple_of(pixel_count + at, LANES), LANES)
            near = pl.ds(pl.multiple_of(j * LANES, LANES), LANES)
            far = pl.ds(pl.multiple_of(CHUNK_PX + j * LANES, LANES), LANES)
            hx, hy = halves(lanes)
            cx, sx = step_table(hx)
            cy, sy = step_table(hy)
            for a in range(SIDE):
                tc, ts = times((cx[a : a + 1], sx[a : a + 1]), (cy, sy))
                tab_c[0, a * SIDE : (a + 1) * SIDE] = tc
                tab_s[0, a * SIDE : (a + 1) * SIDE] = ts
            re = mref[:, lanes].astype(jnp.float32)
            im = mref[:, late].astype(jnp.float32)
            for s in range(NSHIFT):
                p = tab_c[0, s : s + 1]
                q = tab_s[0, s : s + 1]
                kern[s * refs : (s + 1) * refs, near] = (p * re - q * im).astype(jnp.bfloat16)
                kern[s * refs : (s + 1) * refs, far] = (q * re + p * im).astype(jnp.bfloat16)
            return carry

        lax.fori_loop(0, CHUNK_BLOCKS, lane_block, 0)

    tile = 256

    def add_scores(c):
        def row_block(j, carry):
            at = pl.ds(pl.multiple_of(j * tile, tile), tile)
            scores[at, :] += lax.dot_general(
                kern[at, :],
                rows[c],
                (((1,), (1,)), ((), ())),
                preferred_element_type=jnp.float32,
            )
            return carry

        lax.fori_loop(0, NSHIFT * refs // tile, row_block, 0, unroll=2)

    def gather_step(t, carry):
        @pl.when(t + AHEAD < N_CHUNK)
        def _():
            for kind in range(3):
                row_copy(kind, t + AHEAD).start()

        @pl.when(t < N_CHUNK)
        def _():
            row_copy(0, t).wait_recv()
            row_copy(3, t).start()
            row_copy(5, t).start()
            row_copy(1, t).wait_recv()
            row_copy(4, t).start()
            row_copy(6, t).start()

        @pl.when((t >= 1) & (t < N_CHUNK + 1))
        def _():
            row_copy(3, t - 1).wait_recv()
            row_copy(7, t - 1).start()
            row_copy(4, t - 1).wait_recv()
            row_copy(8, t - 1).start()

        @pl.when(t + AHEAD + 1 < N_CHUNK)
        def _():
            center_chunk(t + AHEAD + 1)

        @pl.when(t >= 2)
        def _():
            c = t - 2
            make_kernels(c)
            for kind in (2, 5, 6, 7, 8):
                row_copy(kind, c).wait_recv()
            add_scores(c)

        return carry

    lax.fori_loop(0, N_CHUNK + 2, gather_step, 0)

    scale = 2.0 / math.sqrt(pixel_count)
    top = jnp.max(scores[...], axis=0, keepdims=True) * scale
    total = jnp.sum(jnp.exp(scores[...] * scale - top), axis=0, keepdims=True)
    lbuf[me] = top + jnp.log(total)
    for k in range(1, n_ori):
        lse_copy(k).start()

    seen = facts[...]
    for k in range(1, n_ori):
        fact_copy(k).wait_recv()
        seen = seen + fbuf[k]
    first, second, row_class = seen[0:1], seen[1:2], seen[2:3]
    mine = (first == me) | (second == me)

    for k in range(1, n_ori):
        lse_copy(k).wait_recv()
    peak = jnp.full(first.shape, -jnp.inf, jnp.float32)
    for o in range(n_ori):
        peak = jnp.where((first == o) | (second == o), jnp.maximum(peak, lbuf[o]), peak)
    mass = jnp.zeros(first.shape, jnp.float32)
    for o in range(n_ori):
        mass += jnp.where((first == o) | (second == o), jnp.exp(lbuf[o] - peak), 0.0)
    evidence = peak + jnp.log(mass)
    ev_out[...] = evidence

    def weigh(s, per_ref):
        near = pl.ds(pl.multiple_of(s * refs, refs), refs)
        far = pl.ds(pl.multiple_of((NSHIFT - 1 - s) * refs, refs), refs)
        ahead = jnp.where(mine, jnp.exp(scores[near, :] * scale - evidence), 0.0)
        behind = jnp.where(mine, jnp.exp(scores[far, :] * scale - evidence), 0.0)
        both = ahead + behind
        wp[near, :] = both.astype(jnp.bfloat16)
        wm[near, :] = (ahead - behind).astype(jnp.bfloat16)
        return per_ref + both

    per_ref = lax.fori_loop(
        0, HALF, weigh, jnp.zeros((refs, scores.shape[1]), jnp.float32), unroll=4
    )
    class_rows = lax.broadcasted_iota(jnp.int32, (LANES, scores.shape[1]), 0)
    picks = (class_rows == row_class).astype(jnp.float32)
    cbuf[0] = lax.dot_general(
        per_ref,
        picks,
        (((1,), (1,)), ((), ())),
        precision=lax.Precision.HIGHEST,
        preferred_element_type=jnp.float32,
    )

    def back_block(i, b, h):
        j = h * (n_grp * 8) + i * PIECE_BLOCKS + b
        c = j // CHUNK_BLOCKS
        off = lax.rem(j, CHUNK_BLOCKS) * LANES
        lanes = pl.ds(pl.multiple_of(j * LANES, LANES), LANES)
        hx, hy = halves(lanes)
        cx, sx = times(step_table(hx), hx)
        cy, sy = times(step_table(hy), hy)
        for a in range(SIDE // 2):
            tc, ts = times((cx[a : a + 1], sx[a : a + 1]), (cy, sy))
            tab_c[h, a * SIDE : (a + 1) * SIDE] = tc
            tab_s[h, a * SIDE : (a + 1) * SIDE] = ts
        panel = jnp.concatenate(
            [
                rows[c, :, pl.ds(pl.multiple_of(off, LANES), LANES)],
                rows[c, :, pl.ds(pl.multiple_of(CHUNK_PX + off, LANES), LANES)],
            ],
            axis=1,
        )
        even = jnp.dot(wp[...], panel, preferred_element_type=jnp.float32)
        odd = jnp.dot(wm[...], panel, preferred_element_type=jnp.float32)
        re = jnp.zeros((refs, LANES), jnp.float32)
        im = jnp.zeros((refs, LANES), jnp.float32)
        for s in range(HALF):
            p = tab_c[h, s : s + 1]
            q = tab_s[h, s : s + 1]
            e = even[s * refs : (s + 1) * refs]
            o = odd[s * refs : (s + 1) * refs]
            re += p * e[:, :LANES] + q * o[:, LANES:]
            im += p * e[:, LANES:] - q * o[:, :LANES]
        hc, hs = times(hx, hy)
        at = pl.ds(pl.multiple_of(b * LANES, LANES), LANES)
        for d, sums in ((h, hc * re - hs * im), (2 + h, hc * im + hs * re)):
            part[i, d, :, at] = sums
            sent[i, d, :, at] = sums.astype(jnp.bfloat16)

    def back_piece(i, carry):
        def one(n, inner):
            back_block(i, n, 0)
            back_block(i, n, 1)
            return inner

        lax.fori_loop(0, PIECE_BLOCKS, one, 0)

        @pl.when(i == 0)
        def _():
            for k in range(1, n_grp):
                class_copy(k).start()

        @pl.when(i > 0)
        def _():
            for k in range(1, n_grp):
                back_copy(k, i - 1).start()

        return carry

    lax.fori_loop(0, PIECES, back_piece, 0)
    for k in range(1, n_grp):
        back_copy(k, PIECES - 1).start()

    for k in range(1, n_grp):
        class_copy(k).wait_recv()
    class_out[...] = (cbuf[0] + cbuf[1]) + (cbuf[2] + cbuf[3])

    wide = PIECE_BLOCKS * LANES

    def finish(i, carry):
        for k in range(1, n_grp):
            back_copy(k, i).wait_recv()
        at = pl.ds(pl.multiple_of(i * wide, LANES), wide)
        got = [rbuf[k, i].astype(jnp.float32) for k in range(1, n_grp)]
        back_out[:, at] = (part[i, g] + got[0]) + (got[1] + got[2])
        for k in range(1, n_grp):
            back_copy(k, i).wait_send()
        return carry

    lax.fori_loop(0, PIECES, finish, 0)

    def drain(c, carry):
        for kind in range(9):
            row_copy(kind, c).wait_send()
        return carry

    lax.fori_loop(0, N_CHUNK, drain, 0)
    for k in range(1, n_ori):
        fact_copy(k).wait_send()
        lse_copy(k).wait_send()
    for k in range(1, n_grp):
        class_copy(k).wait_send()


def per_device_fused(particles, priors, offsets, classes, ctf_table, references):
    n_ori = lax.axis_size("ori")
    n_grp = lax.axis_size("grp")
    me = lax.axis_index("ori")
    g = lax.axis_index("grp")
    per = priors.shape[0]
    refs = references.shape[0]
    n_rows = n_ori * per
    hyps = NSHIFT * refs
    info = jnp.stack([classes, offsets[0], offsets[1]], axis=1)
    listed = jnp.stack([priors[:, 0], priors[:, 1], classes])
    listed = jnp.pad(listed, ((0, 5), (0, 0)))
    placed = jnp.tile(listed, (1, n_ori))
    facts = jnp.where(jnp.arange(n_rows)[None, :] // per == me, placed, 0)
    wide = PIECES * PIECE_BLOCKS * LANES
    vmem = pl.BlockSpec(memory_space=pltpu.VMEM)
    sems = pltpu.SemaphoreType.DMA
    back, by_class, evidence = pl.pallas_call(
        functools.partial(fused_kernel, n_ori, n_grp),
        out_shape=[
            jax.ShapeDtypeStruct((refs, wide), jnp.float32),
            jax.ShapeDtypeStruct((refs, LANES), jnp.float32),
            jax.ShapeDtypeStruct((1, n_rows), jnp.float32),
        ],
        in_specs=[vmem] * 5,
        out_specs=[vmem] * 3,
        scratch_shapes=[
            pltpu.VMEM((N_CHUNK, n_rows, 2 * CHUNK_PX), jnp.bfloat16),
            pltpu.VMEM((hyps, 2 * CHUNK_PX), jnp.bfloat16),
            pltpu.VMEM((hyps, n_rows), jnp.float32),
            pltpu.VMEM((hyps // 2, n_rows), jnp.bfloat16),
            pltpu.VMEM((hyps // 2, n_rows), jnp.bfloat16),
            pltpu.VMEM((2, NSHIFT, LANES), jnp.float32),
            pltpu.VMEM((2, NSHIFT, LANES), jnp.float32),
            pltpu.VMEM((n_ori, 8, n_rows), jnp.int32),
            pltpu.VMEM((n_ori, 1, n_rows), jnp.float32),
            pltpu.VMEM((n_grp, refs, LANES), jnp.float32),
            pltpu.VMEM((PIECES, n_grp, refs, PIECE_BLOCKS * LANES), jnp.float32),
            pltpu.VMEM((PIECES, n_grp, refs, PIECE_BLOCKS * LANES), jnp.bfloat16),
            pltpu.VMEM((n_grp, PIECES, refs, PIECE_BLOCKS * LANES), jnp.bfloat16),
            pltpu.VMEM((4, pixel_count), jnp.float32),
            sems((9, N_CHUNK)),
            sems((9, N_CHUNK)),
            sems((n_ori,)),
            sems((n_ori,)),
            sems((n_ori,)),
            sems((n_ori,)),
            sems((n_grp,)),
            sems((n_grp,)),
            sems((n_grp, PIECES)),
            sems((n_grp, PIECES)),
        ],
        compiler_params=pltpu.CompilerParams(
            collective_id=0, has_side_effects=True, vmem_limit_bytes=56 * 2**20
        ),
    )(particles, info, facts, ctf_table, references)

    n_classes = ctf_table.shape[0]
    width = pixel_count // n_grp
    table_part = lax.dynamic_slice_in_dim(ctf_table, g * width, width, 1)
    weight_part = jnp.dot(
        by_class[:, :n_classes], table_part * table_part, precision=lax.Precision.HIGHEST
    )
    cols = 2 * width
    back_part = jnp.where(g % 2 == 0, back[:, :cols], back[:, wide - cols :])
    own = lax.dynamic_slice_in_dim(evidence[0], me * per, per, 0)
    return (back_part, weight_part, own)


def solution(mesh):
    small = mesh.shape["ori"] == 8 and mesh.shape["grp"] == 4
    per_device = per_device_fused if small else per_device_plain
    placed = (
        P(("grp", "ori"), None),
        P(("grp", "ori"), None),
        P(None, ("grp", "ori")),
        P(("grp", "ori")),
        P(),
        P("ori", None),
    )
    return jax.shard_map(
        per_device,
        mesh=mesh,
        in_specs=placed,
        out_specs=(P("ori", "grp"), P("ori", "grp"), P(("grp", "ori"))),
        check_vma=False,
    )
```
